32 devices in a mesh: groups: 2 (over x), chan: 8 (over z, y), seq: 2 (over core).
Axes of the slice: x: 2, y: 2, z: 4, core: 2. Of those that a mesh axis runs over, the one named last changes fastest.
Arguments:
- tokens: bfloat16 [2048, 8192], P(('groups', 'seq'), 'chan'), parts along dimension 0, may hold values from -42 to 42
- norm_gain: float32 [8192], replicated, may hold values from 0.1 to 1.9
- in_weight: bfloat16 [3, 8192, 8192], P(None, None, 'chan'), may hold values from -0.0625 to 0.0625
- short_weight: float32 [3, 7, 8192], P(None, None, 'chan'), may hold values from -2 to 2
- log_decay: float32 [16, 8192], P(None, 'chan'), may hold values from -0.034 to 0
- residue: float32 [16, 8192], P(None, 'chan'), may hold values from -0.15625 to 0.15625
- skip: float32 [8192], P('chan'), may hold values from 0.1 to 1.9
- out_weight: bfloat16 [8192, 8192], P('chan'), may hold values from -0.09375 to 0.09375
Outputs:
- mixed: bfloat16 [2048, 8192], P(('groups', 'seq'), 'chan'), parts along dimension 0
The draws below stay inside these ranges and needn't reach their ends.
There are 2 independent parts, one for each index of `groups`. The reference program is written for one: setup_inputs(seed, part) draws one part's arguments, and reference() takes and returns one part's arrays. A program takes and returns all parts, laid end to end along the dimension named above; an argument that names none is the same for every part. Nothing has to cross between parts.
All inputs are finite; a program needn't handle non-finite values.
Results may differ from the reference program's by a relative error of at most 0.0067.
Values may be sent and summed in bfloat16 or wider, within the bound.
A program may use at most 448 MiB of HBM per device.

```python
import math
import jax
import jax.numpy as jnp
from jax import lax

D = 8192
POLES = 16
SHORT = 7
SEQ_LEN = 1024


def draw_tokens(key, part):
    keys = jax.random.split(key, 3)
    row_scale = jnp.exp(jax.random.uniform(keys[1], (SEQ_LEN, 1), jnp.float32, math.log(0.3), math.log(3.0)))
    ramp = jnp.sqrt(1.0 + 2.0 * jnp.arange(D, dtype=jnp.float32) / D)
    col_scale = jnp.exp(jax.random.uniform(keys[2], (1, D), jnp.float32, math.log(0.5), math.log(2.0))) * ramp[None, :]
    base = jnp.clip(jax.random.normal(keys[0], (SEQ_LEN, D), jnp.float32), -4.0, 4.0)
    return (base * row_scale * col_scale).astype(jnp.bfloat16)


def draw_log_decay(key, part):
    keys = jax.random.split(key, 3)
    slow = jnp.exp(jax.random.uniform(keys[0], (POLES, D), jnp.float32, math.log(0.1 / SEQ_LEN), math.log(2.0 / SEQ_LEN)))
    fast = jnp.exp(jax.random.uniform(keys[1], (POLES, D), jnp.float32, math.log(1.0 / 50.0), math.log(1.0 / 30.0)))
    share = 0.5
    picked = jax.random.uniform(keys[2], (POLES, D), jnp.float32) < share
    return -jnp.where(picked, fast, slow)


def with_spikes(drawn, own_key, source, target, shards_of, factor):
    def block_of(dim):
        return (jnp.arange(drawn.shape[dim]) // (drawn.shape[dim] // shards_of)).reshape((-1,) + (1,) * (drawn.ndim - 1 - dim))

    near = jax.random.permutation(own_key, shards_of)[block_of(target)]
    second = (block_of(target) + shards_of // 2) % shards_of
    return jnp.where((block_of(source) == near) | (block_of(source) == second), factor * drawn, drawn)


def block_levels(own_key, shape, shards, smallest, largest):
    factor_of = 1.0
    for dim, blocks in shards:
        steps = jax.random.uniform(jax.random.fold_in(jax.random.fold_in(own_key, 6), dim), (blocks,), jnp.float32, smallest / len(shards), largest / len(shards))
        factor_of = factor_of * jnp.repeat(jnp.exp(steps), shape[dim] // blocks).reshape((-1,) + (1,) * (len(shape) - 1 - dim))
    return factor_of


def gaussian(key, extent, spread, reach, shards=(), kind=jnp.bfloat16):
    values = spread * jax.random.normal(key, extent, jnp.float32)
    if shards:
        values = values * block_levels(key, extent, shards, -0.22, 0.18)
    return jnp.clip(values, -reach, reach).astype(kind)


def noise_with(key, extent, spread, most, cuts, heavy, held_as=jnp.bfloat16):
    array = spread * jax.random.normal(key, extent, jnp.float32)
    if cuts:
        array = array * block_levels(key, extent, cuts, -0.22, 0.18)
    return jnp.clip(with_spikes(array, jax.random.fold_in(key, 3), *heavy), -most, most).astype(held_as)


def setup_inputs(seed: int = 0, part: int = 0) -> dict:
    splits = jax.random.split(jax.random.key(seed), 9)
    own_keys = jax.random.split(jax.random.fold_in(splits[8], part), 9)
    return {
        "tokens": draw_tokens(jax.random.fold_in(jax.random.fold_in(splits[8], part), 71), part),
        "norm_gain": jnp.clip(1.0 + 0.18 * jax.random.normal(splits[1], (D,), jnp.float32), 0.1, 1.9),
        "in_weight": gaussian(splits[2], (3, D, D), D ** -0.5, 0.0625, ((2, 8),)),
        "short_weight": gaussian(splits[3], (3, SHORT, D), SHORT ** -0.5, 2.0, ((2, 8),), jnp.float32),
        "log_decay": draw_log_decay(jax.random.fold_in(splits[8], 71), part),
        "residue": gaussian(splits[5], (POLES, D), ((2.0 / (POLES * SEQ_LEN)) ** 0.5), 0.15625, ((1, 8),), jnp.float32),
        "skip": jnp.clip(1.0 + 0.18 * jax.random.normal(splits[6], (D,), jnp.float32), 0.1, 1.9),
        "out_weight": noise_with(splits[7], (D, D), D ** -0.5, 0.09375, ((0, 8),), (0, 1, 8, 2.0)),
    }


EPSILON = 1e-06

def reference(tokens, norm_gain, in_weight, short_weight, log_decay, residue, skip, out_weight):
    seq_total = tokens.shape[0]
    taps = short_weight.shape[1]
    tok_float = tokens.astype(jnp.float32)
    inv_rms = lax.rsqrt(lax.optimization_barrier(jnp.mean(tok_float * tok_float, axis=1, keepdims=True)) + EPSILON)
    scaled = (tok_float * norm_gain[None, :]).astype(jnp.bfloat16)
    proj = jnp.stack([(jnp.dot(scaled, in_weight[which], preferred_element_type=jnp.float32) * inv_rms).astype(jnp.bfloat16) for which in range(3)])
    proj_float = proj.astype(jnp.float32)
    padded = jnp.pad(proj_float, ((0, 0), (taps - 1, 0), (0, 0)))
    conv = jnp.zeros_like(proj_float)
    for tap in range(taps):
        conv = conv + short_weight[:, tap][:, None, :] * padded[:, taps - 1 - tap:taps - 1 - tap + seq_total, :]
    query = conv[0]
    product = conv[1] * conv[2]
    poles = jnp.exp(log_decay)

    def advance(state, row):
        state = poles * state + row[None, :]
        return (state, lax.optimization_barrier(jnp.sum(residue * state, axis=0)))
    _, long_conv = lax.scan(advance, jnp.zeros(log_decay.shape, jnp.float32), product)
    gated = (query * (long_conv + skip[None, :] * product)).astype(jnp.bfloat16)
    return (tok_float + jnp.dot(gated, out_weight, preferred_element_type=jnp.float32)).astype(jnp.bfloat16)
```

```python
import functools

import jax
import jax.numpy as jnp
from jax import lax
from jax.experimental import pallas as pl
from jax.experimental.pallas import tpu as pltpu
from jax.sharding import PartitionSpec as P

EPSILON = 1e-06
MESH = pl.DeviceIdType.MESH
PIECES = 4
W_SLOTS = 4


def ring_position(index, n):
    odd = lax.rem(index, 2)
    return (1 - odd) * lax.div(index, 2) + odd * (n - 1 - lax.div(index, 2))


def ring_index(position, n):
    back = lax.div(position, n // 2)
    return (1 - back) * (2 * position) + back * (2 * (n - 1 - position) + 1)


def greet(peers):
    barrier = pltpu.get_barrier_semaphore()
    for peer in peers:
        pl.semaphore_signal(barrier, inc=1, device_id=peer, device_id_type=MESH)
    pl.semaphore_wait(barrier, len(peers))


def strided(start, size, stride):
    return pl.ds(start, size) if stride == 1 else pl.ds(start, size, stride=stride)


def front_kernel(
    n, eps, tok_hbm, gain_ref, w_hbm, taps_ref, decay_ref, res_ref, skip_ref, gated_ref,
    held, acc, w_buf, scaled, squares, query, signal_rows, pole, residue, skip_rows,
    rim_out, rim_in, state_out, state_in, first_state, send_sem, recv_sem, w_sem, own_sem, pair_send, pair_recv, turn,
):
    rows, width = tok_hbm.shape
    middle = n // 2
    piece = rows // PIECES
    groups = width // 128
    poles = decay_ref.shape[0]
    tap_count = taps_ref.shape[1]
    chunk = min(64, rows)
    tile = min(256, width)
    me = lax.axis_index("chan")
    seq = lax.axis_index("seq")
    pos = ring_position(me, n)
    right = {"chan": ring_index(lax.rem(pos + 1, n), n)}
    left = {"chan": ring_index(lax.rem(pos + n - 1, n), n)}
    partner = {"seq": 1 - seq}
    ahead = (right, left)

    def owner_of(block):
        away = lax.div(block + 1, 2)
        odd = lax.rem(block, 2)
        return ring_index(lax.rem(pos + odd * (n - away) + (1 - odd) * away, n), n)

    def w_copy(g):
        owner = owner_of(lax.div(g, 3))
        slot = lax.rem(g, W_SLOTS)
        return pltpu.make_async_copy(
            w_hbm.at[lax.rem(g, 3), pl.ds(pl.multiple_of(owner * width, 128), width), :],
            w_buf.at[slot],
            w_sem.at[slot],
        )

    def hop(direction, step, part, away):
        shift = pos + n - away if direction == 0 else pos + away
        owner = ring_index(lax.rem(shift, n), n)
        span = pl.ds(part * piece, piece)
        return pltpu.make_async_remote_copy(
            src_ref=held.at[owner, span, :],
            dst_ref=held.at[owner, span, :],
            send_sem=send_sem.at[direction, step, part],
            recv_sem=recv_sem.at[direction, step, part],
            device_id=ahead[direction],
            device_id_type=MESH,
        )

    own = pltpu.make_async_copy(tok_hbm, held.at[me], own_sem)
    own.start()
    for g in range(W_SLOTS):
        w_copy(jnp.int32(g)).start()
    greet((right, left, partner))
    own.wait()

    @pl.when(seq > 0)
    def _():
        pl.semaphore_wait(turn, 1)

    for part in range(PIECES):
        for direction in range(2):
            hop(direction, 0, part, 0).start()

    @pl.loop(0, rows // chunk)
    def _(b):
        r = pl.multiple_of(b * chunk, chunk)
        squares[pl.ds(r, chunk), :] = jnp.zeros((chunk, 128), jnp.float32)
        for i in range(3):
            acc[i, pl.ds(r + 8, chunk), :] = jnp.zeros((chunk, width), jnp.float32)

    for j in range(groups):
        lanes = pl.ds(j * 128, 128)
        pole[strided(j, poles, groups), :] = jnp.exp(decay_ref[:, lanes])
        residue[strided(j, poles, groups), :] = res_ref[:, lanes]
        skip_rows[pl.ds(j, 1), :] = skip_ref[:, lanes]

    def prepare(block):
        owner = owner_of(block)
        gain = gain_ref[:, pl.ds(pl.multiple_of(owner * width, 128), width)]
        small = min(32, rows)

        @pl.loop(0, rows // small)
        def _(b):
            r = pl.multiple_of(b * small, small)
            x = held[owner, pl.ds(r, small), :].astype(jnp.float32)
            scaled[pl.ds(r, small), :] = (x * gain).astype(jnp.bfloat16)
            total = squares[pl.ds(r, small), :]
            for j in range(groups):
                xj = x[:, j * 128 : (j + 1) * 128]
                total = total + xj * xj
            squares[pl.ds(r, small), :] = total

    def multiply(block, i):
        g = block * 3 + i
        slot = lax.rem(g, W_SLOTS)
        w_copy(g).wait()

        @pl.loop(0, width // tile)
        def _(c):
            cols = pl.ds(pl.multiple_of(c * tile, 128), tile)
            acc[i, pl.ds(8, rows), cols] += jnp.dot(
                scaled[...], w_buf[slot, :, cols], preferred_element_type=jnp.float32
            )

        @pl.when(g + W_SLOTS < n * 3)
        def _():
            w_copy(g + W_SLOTS).start()

    def arrive(step, part):
        for direction in range(2):
            hop(direction, step - 1, part, step).wait_recv()
            if part // (PIECES // 2) == direction:
                hop(direction, step, part, step).start()
            else:

                @pl.when(step < middle - 1)
                def _():
                    hop(direction, step, part, step).start()

    def pair_part(step, quarter):
        near = 2 * step - 1
        if quarter == 0:
            prepare(near)
            multiply(near, 0)
            multiply(near, 1)
        elif quarter == 1:
            multiply(near, 2)
        elif quarter == 2:
            prepare(near + 1)
            multiply(near + 1, 0)
            multiply(near + 1, 1)
        else:
            multiply(near + 1, 2)

    for part in range(PIECES):
        arrive(jnp.int32(1), part)
        if part == 0:
            prepare(jnp.int32(0))
        if part < 3:
            multiply(jnp.int32(0), part)

    @pl.loop(2, middle)
    def _(step):
        for part in range(PIECES):
            arrive(step, part)
            pair_part(step - 1, part)

    @pl.when(seq == 0)
    def _():
        pl.semaphore_signal(turn, inc=1, device_id=partner, device_id_type=MESH)

    for part in range(PIECES):
        pair_part(jnp.int32(middle - 1), part)
    for part in range(PIECES):
        hop(part // (PIECES // 2), middle - 1, part, middle).wait_recv()
    prepare(jnp.int32(n - 1))
    for i in range(3):
        multiply(jnp.int32(n - 1), i)

    @pl.loop(0, rows // chunk)
    def _(b):
        r = pl.multiple_of(b * chunk, chunk)
        mean = jnp.sum(squares[pl.ds(r, chunk), :], axis=1, keepdims=True) / (n * width)
        inv = lax.rsqrt(mean + eps)
        for i in range(3):
            span = pl.ds(r + 8, chunk)
            acc[i, span, :] = (acc[i, span, :] * inv).astype(jnp.bfloat16).astype(jnp.float32)

    rim_out[...] = acc[:, pl.ds(rows, 8), :]
    rim = pltpu.make_async_remote_copy(
        src_ref=rim_out, dst_ref=rim_in, send_sem=pair_send.at[0], recv_sem=pair_recv.at[0],
        device_id=partner, device_id_type=MESH,
    )

    @pl.when(seq == 0)
    def _():
        rim.start()

    @pl.when(seq > 0)
    def _():
        rim.wait_recv()

    acc[:, pl.ds(0, 8), :] = jnp.zeros((3, 8, width), jnp.float32)

    @pl.when(seq > 0)
    def _():
        acc[:, pl.ds(0, 8), :] = rim_in[...]


    @pl.loop(0, groups)
    def _(j):
        lanes = pl.ds(pl.multiple_of(j * 128, 128), 128)

        @pl.loop(0, rows // chunk)
        def _(b):
            r = pl.multiple_of(b * chunk, chunk)
            conv = []
            for i in range(3):
                x = acc[i, pl.ds(r, chunk + 8), lanes]
                total = x[8:, :] * taps_ref[i, pl.ds(0, 1), lanes]
                for tap in range(1, tap_count):
                    shifted = pltpu.roll(x, tap, 0)[8:, :]
                    total = total + shifted * taps_ref[i, pl.ds(tap, 1), lanes]
                conv.append(total)
            query[pl.ds(r, chunk), lanes] = conv[0]
            signal_rows[strided(r * groups + j, chunk, groups), :] = conv[1] * conv[2]

    def row_at(t):
        return pl.ds(pl.multiple_of(t * groups, groups), groups)

    poles_held = [pole[pl.ds(k * groups, groups), :] for k in range(poles)]

    carry = pltpu.make_async_remote_copy(
        src_ref=state_out, dst_ref=state_in, send_sem=pair_send.at[1], recv_sem=pair_recv.at[1],
        device_id=partner, device_id_type=MESH,
    )
    entry_rows = poles * groups

    @pl.when(seq == 0)
    def _():
        first_state[...] = jnp.zeros((entry_rows, 128), jnp.float32)

    @pl.when(seq > 0)
    def _():
        carry.wait_recv()
        first_state[...] = state_in[...]

    res_held = [residue[pl.ds(k * groups, groups), :] for k in range(poles)]
    skip_held = skip_rows[...]

    def with_output(t, state):
        row = signal_rows[row_at(t), :]
        state = tuple(poles_held[k] * state[k] + row for k in range(poles))
        terms = [res_held[k] * state[k] for k in range(poles)]
        while len(terms) > 1:
            terms = [a + b for a, b in zip(terms[::2], terms[1::2])] + terms[len(terms) // 2 * 2 :]
        signal_rows[row_at(t), :] = terms[0] + skip_held * row
        return state

    entry = tuple(first_state[pl.ds(k * groups, groups), :] for k in range(poles))
    last = lax.fori_loop(0, rows, with_output, entry, unroll=4)
    for k in range(poles):
        state_out[pl.ds(k * groups, groups), :] = last[k]

    @pl.when(seq == 0)
    def _():
        carry.start()

    @pl.loop(0, groups)
    def _(j):
        lanes = pl.ds(pl.multiple_of(j * 128, 128), 128)

        @pl.loop(0, rows // chunk)
        def _(b):
            r = pl.multiple_of(b * chunk, chunk)
            long = signal_rows[strided(r * groups + j, chunk, groups), :]
            gated_ref[pl.ds(r, chunk), lanes] = (query[pl.ds(r, chunk), lanes] * long).astype(jnp.bfloat16)

    @pl.when(seq == 0)
    def _():
        rim.wait_send()
        carry.wait_send()

    for part in range(PIECES):
        for direction in range(2):

            @pl.loop(0, middle - 1)
            def _(step):
                hop(direction, step, part, step).wait_send()

        hop(part // (PIECES // 2), middle - 1, part, middle - 1).wait_send()


def back_kernel(
    n, gated_ref, tok_ref, w_hbm, out_ref, w_buf, partial, outgoing, incoming, send_sem, recv_sem, w_sem
):
    rows, width = tok_ref.shape
    middle = n // 2
    piece = rows // PIECES
    small = min(32, piece)
    tile = min(256, width)
    me = lax.axis_index("chan")
    pos = ring_position(me, n)
    right = {"chan": ring_index(lax.rem(pos + 1, n), n)}
    left = {"chan": ring_index(lax.rem(pos + n - 1, n), n)}
    ahead = (right, left)

    def w_copy(block):
        away = middle - lax.div(block + 1, 2)
        odd = lax.rem(block, 2)
        target = ring_index(lax.rem(pos + odd * away + (1 - odd) * (n - away), n), n)
        slot = lax.rem(block, W_SLOTS)
        return pltpu.make_async_copy(
            w_hbm.at[:, pl.ds(pl.multiple_of(target * width, 128), width)],
            w_buf.at[slot],
            w_sem.at[slot],
        )

    def hop(direction, step, part):
        span = pl.ds(part * piece, piece)
        return pltpu.make_async_remote_copy(
            src_ref=outgoing.at[direction, step, span, :],
            dst_ref=incoming.at[direction, step, span, :],
            send_sem=send_sem.at[direction, step, part],
            recv_sem=recv_sem.at[direction, step, part],
            device_id=ahead[direction],
            device_id_type=MESH,
        )

    def multiply(block, place):
        slot = lax.rem(block, W_SLOTS)
        w_copy(block).wait()

        @pl.loop(0, width // tile)
        def _(c):
            cols = pl.ds(pl.multiple_of(c * tile, 128), tile)
            partial[place, :, cols] = jnp.dot(
                gated_ref[...], w_buf[slot, :, cols], preferred_element_type=jnp.float32
            )

        @pl.when(block + W_SLOTS < n)
        def _():
            w_copy(block + W_SLOTS).start()

    def send(direction, step, part, place, add):
        @pl.loop(0, piece // small)
        def _(b):
            span = pl.ds(pl.multiple_of(part * piece + b * small, small), small)
            total = partial[place, span, :]
            if add:
                total = total + incoming[direction, step - 1, span, :].astype(jnp.float32)
            outgoing[direction, step, span, :] = total.astype(jnp.bfloat16)

        hop(direction, step, part).start()

    def side(part):
        return part // (PIECES // 2)

    order = [k // 2 + (k % 2) * (PIECES // 2) for k in range(PIECES)]
    for block in range(W_SLOTS):
        w_copy(jnp.int32(block)).start()
    greet((right, left))
    multiply(jnp.int32(0), 0)
    for part in order:
        send(side(part), 0, part, 0, False)
    for direction in range(2):
        multiply(jnp.int32(1 + direction), direction)
    for direction in range(2):
        for part in range(PIECES):
            if side(part) != direction:
                send(direction, 1, part, direction, False)
    for part in order:
        hop(side(part), 0, part).wait_recv()
        send(side(part), 1, part, side(part), True)

    @pl.loop(2, middle)
    def _(step):
        for direction in range(2):
            multiply(2 * step - 1 + direction, direction)
        for k in range(PIECES):
            for direction in range(2):
                part = (k + (1 - direction) * (PIECES // 2)) % PIECES
                hop(direction, step - 1, part).wait_recv()
                send(direction, step, part, direction, True)

    multiply(jnp.int32(n - 1), 0)
    for part in range(PIECES):
        for direction in range(2):
            hop(direction, middle - 1, part).wait_recv()

        @pl.loop(0, piece // small)
        def _(b):
            span = pl.ds(pl.multiple_of(part * piece + b * small, small), small)
            total = partial[0, span, :]
            for direction in range(2):
                total = total + incoming[direction, middle - 1, span, :].astype(jnp.float32)
            out_ref[span, :] = (tok_ref[span, :].astype(jnp.float32) + total).astype(jnp.bfloat16)

    for part in range(PIECES):
        hop(side(part), 0, part).wait_send()
        for direction in range(2):

            @pl.loop(1, middle)
            def _(step):
                hop(direction, step, part).wait_send()


def grid_kernel(
    n, eps, tok_hbm, gain_ref, in_hbm, taps_ref, decay_ref, res_ref, skip_ref, out_w_hbm, out_ref,
    held, work, w_buf, outgoing, rows_here, gated, scaled, squares, signal_rows, pole, residue, skip_rows, state_rows,
    send_sem, recv_sem, w_sem, local_sem, tok_send, tok_recv, gate_send, gate_recv, back_send, back_recv,
):
    rows, width = tok_hbm.shape
    chunk_rows = rows // 2
    chunks = 4
    line = n // 2
    groups = width // 128
    poles = decay_ref.shape[0]
    tap_count = taps_ref.shape[1]
    small = 16
    batch = min(64, chunk_rows)
    f32, bf16 = jnp.float32, jnp.bfloat16
    pieces = route_pieces(chunk_rows)
    me = lax.axis_index("chan")
    seq = lax.axis_index("seq")
    z = lax.div(me, 2)
    y = lax.rem(me, 2)
    across = 1 - y
    partner = {"seq": 1 - seq}
    has_low = z > 0
    has_high = z < line - 1
    edge = jnp.logical_or(z == 0, z == line - 1)
    middle = jnp.logical_and(has_low, has_high)
    mid = lax.div(z * (3 - z), 2)
    high = lax.div(z, 2)

    def place(j):
        wrap = lax.div(j, 3)
        near = (1 - mid) * j + mid * ((1 - wrap) * lax.rem(j + 1, 3) + 3 * wrap)
        return (1 - high) * near + high * (3 - near)

    def above(target):
        return lax.div(target - z + 3, 4)

    def chip(row, column):
        return {"chan": row * 2 + column}

    def span_of(p):
        return pl.ds(pieces[p][0], pieces[p][1])

    def each(kind, flexible, act):
        for p, (_, _, route) in enumerate(pieces):
            if route == kind:
                act(p)
            elif route == "either":
                pred = flexible if kind == "line" else jnp.logical_not(flexible)

                @pl.when(pred)
                def _():
                    act(p)

    def remote(src, dst, way, k, block, p, device):
        return pltpu.make_async_remote_copy(
            src_ref=src, dst_ref=dst, send_sem=send_sem.at[way, k, block, p], recv_sem=recv_sem.at[way, k, block, p],
            device_id=device, device_id_type=MESH,
        )

    def arrived(way, k, block, p):
        here = held.at[k, block, span_of(p), :]
        remote(here, here, way, k, block, p, chip(z, across)).wait_recv()

    def token_copy(half):
        return pltpu.make_async_remote_copy(
            src_ref=tok_hbm.at[pl.ds(half * chunk_rows, chunk_rows), :],
            dst_ref=held.at[2 + half, me],
            send_sem=tok_send.at[half], recv_sem=tok_recv.at[half], device_id=partner, device_id_type=MESH,
        )

    def residual_copy(half):
        return pltpu.make_async_remote_copy(
            src_ref=tok_hbm.at[pl.ds(half * chunk_rows, chunk_rows), :],
            dst_ref=rows_here.at[half],
            send_sem=tok_send.at[half], recv_sem=tok_recv.at[half], device_id=partner, device_id_type=MESH,
        )

    def gate_copy(k):
        return pltpu.make_async_remote_copy(
            src_ref=gated.at[k], dst_ref=gated.at[k], send_sem=gate_send.at[k], recv_sem=gate_recv.at[k],
            device_id=partner, device_id_type=MESH,
        )

    def result_copy(k):
        return pltpu.make_async_remote_copy(
            src_ref=rows_here.at[k], dst_ref=rows_here.at[k], send_sem=back_send.at[k], recv_sem=back_recv.at[k],
            device_id=partner, device_id_type=MESH,
        )

    def greet_all():
        barrier = pltpu.get_barrier_semaphore()

        def hello(device):
            pl.semaphore_signal(barrier, inc=1, device_id=device, device_id_type=MESH)

        hello(partner)
        hello(chip(z, across))

        @pl.when(has_low)
        def _():
            hello(chip(z - 1, y))

        @pl.when(has_high)
        def _():
            hello(chip(z + 1, y))

        pl.semaphore_wait(barrier, 3 + mid)

    def front():
        steps = n * 3

        def flexible(k):
            return k < 1

        def block_at(s):
            even = 1 - lax.rem(s, 2)
            last = lax.div(s, n - 1)
            other = even * lax.div(s + n - 1, n) + last
            own = lax.div(s + 1, 2)
            beside = even * (lax.div(s, 2) - 1) + 3 * last
            j = (1 - other) * own + other * beside
            return place(j) * 2 + (1 - other) * y + other * across

        def w_copy(g):
            inner = lax.rem(g, steps)
            owner = block_at(lax.div(inner, 3))
            slot = lax.rem(g, W_SLOTS)
            return pltpu.make_async_copy(
                in_hbm.at[lax.rem(inner, 3), pl.ds(pl.multiple_of(owner * width, 128), width), :],
                w_buf.at[slot],
                w_sem.at[slot],
            )

        def push(way, k, block, p):
            here = held.at[k, block, span_of(p), :]
            device = (chip(z + 1, y), chip(z - 1, y), chip(z, across))[way]
            return remote(here, here, way, k, block, p, device)

        def along(way, k, block, p):
            here = held.at[k, block, span_of(p), :]
            return remote(here, here, way, k, block, p, chip(z + 1 - 2 * way, y))

        def onward(way):
            following = z + 1 - 2 * way
            return jnp.logical_and(following >= 0, following < line)

        def both_ways(k, block, p, act):
            @pl.when(has_low)
            def _():
                act(push(1, k, block, p))

            @pl.when(has_high)
            def _():
                act(push(0, k, block, p))

        def own_part(k, act):
            for p in range(len(pieces)):
                both_ways(k, me, p, act)
                act(push(2, k, me, p))

        def line_part(k, j, act, wait):
            target = place(j)
            way = above(target)
            block = target * 2 + y

            def first(p):
                if wait:
                    arrived(way, k, block, p)

                @pl.when(onward(way))
                def _():
                    act(along(way, k, block, p))

                act(push(2, k, block, p))

            def second(p):
                if wait:
                    arrived(way, k, block, p)

                @pl.when(onward(way))
                def _():
                    act(along(way, k, block, p))

            each("line", flexible(k), first)
            each("cross", flexible(k), second)

        def cross_part(k, j, act, wait):
            target = place(j)
            way = above(target)
            block = target * 2 + across

            def second(p):
                if wait:
                    arrived(way, k, block, p)

                @pl.when(onward(way))
                def _():
                    act(along(way, k, block, p))

            each("cross", flexible(k), second)

        def cross_start(k, act, wait):
            block = z * 2 + across

            def second(p):
                if wait:
                    arrived(2, k, block, p)
                both_ways(k, block, p, act)

            each("cross", flexible(k), second)

        def start(copy):
            copy.start()

        def finish(copy):
            copy.wait_send()

        own_copies = [
            pltpu.make_async_copy(tok_hbm.at[pl.ds(h * chunk_rows, chunk_rows), :], held.at[h, me], local_sem.at[h])
            for h in range(2)
        ]
        for copy in own_copies:
            copy.start()
        for g in range(W_SLOTS):
            w_copy(jnp.int32(g)).start()
        greet_all()
        own_copies[0].wait()
        own_part(jnp.int32(0), start)
        for half in range(2):
            residual_copy(half).start()
        own_copies[1].wait()

        work[pl.ds(0, 3), :, :] = jnp.zeros((3, chunk_rows + 8, width), f32)
        squares[...] = jnp.zeros((chunk_rows, 128), f32)
        state_rows[...] = jnp.zeros((poles * groups, 128), f32)
        for j in range(groups):
            lanes = pl.ds(j * 128, 128)
            pole[strided(j, poles, groups), :] = jnp.exp(decay_ref[:, lanes])
            residue[strided(j, poles, groups), :] = res_ref[:, lanes]
            skip_rows[pl.ds(j, 1), :] = skip_ref[:, lanes]
        for half in range(2):
            token_copy(half).wait_recv()

        def row_at(t):
            return pl.ds(pl.multiple_of(t * groups, groups), groups)

        @pl.loop(0, chunks)
        def _(k):
            @pl.loop(0, n)
            def _(s):
                odd = lax.rem(s, 2)

                @pl.when(jnp.logical_and(odd == 1, s < n - 1))
                def _():
                    line_part(k, lax.div(s + 1, 2), start, True)

                @pl.when(s == 1)
                def _():
                    cross_start(k, start, True)

                @pl.when(jnp.logical_and(odd == 1, s > 1))
                def _():
                    cross_part(k, lax.div(s - 1, 2), start, True)

                @pl.when(jnp.logical_and(s == 3, k < chunks - 1))
                def _():
                    own_part(k + 1, start)

                @pl.when(jnp.logical_and(odd == 0, s > 0))
                def _():
                    each("line", flexible(k), lambda p: arrived(2, k, place(lax.div(s, 2) - 1) * 2 + across, p))

                @pl.when(s == n - 1)
                def _():
                    each("line", flexible(k), lambda p: arrived(2, k, place(jnp.int32(3)) * 2 + across, p))

                owner = block_at(s)
                gain = gain_ref[:, pl.ds(pl.multiple_of(owner * width, 128), width)]
                part = min(32, chunk_rows)

                @pl.loop(0, chunk_rows // part)
                def _(b):
                    r = pl.multiple_of(b * part, part)
                    x = held[k, owner, pl.ds(r, part), :].astype(f32)
                    scaled[pl.ds(r, part), :] = (x * gain).astype(bf16)
                    total = squares[pl.ds(r, part), :]
                    for j in range(groups):
                        xj = x[:, j * 128 : (j + 1) * 128]
                        total = total + xj * xj
                    squares[pl.ds(r, part), :] = total

                @pl.loop(0, 3)
                def _(i):
                    g = k * steps + s * 3 + i
                    slot = lax.rem(g, W_SLOTS)
                    w_copy(g).wait()
                    work[i, pl.ds(8, chunk_rows), :] += jnp.dot(
                        scaled[...], w_buf[slot], preferred_element_type=f32
                    )

                    @pl.when(g + W_SLOTS < chunks * steps)
                    def _():
                        w_copy(g + W_SLOTS).start()

            @pl.loop(0, chunk_rows // batch)
            def _(b):
                r = pl.multiple_of(b * batch, batch)
                mean = jnp.sum(squares[pl.ds(r, batch), :], axis=1, keepdims=True) / (n * width)
                inv = lax.rsqrt(mean + eps)
                for i in range(3):
                    span = pl.ds(r + 8, batch)
                    work[i, span, :] = (work[i, span, :] * inv).astype(bf16).astype(f32)
                squares[pl.ds(r, batch), :] = jnp.zeros((batch, 128), f32)

            @pl.loop(0, groups)
            def _(j):
                lanes = pl.ds(pl.multiple_of(j * 128, 128), 128)

                @pl.loop(0, chunk_rows // batch)
                def _(b):
                    r = pl.multiple_of(b * batch, batch)
                    conv = []
                    for i in range(3):
                        x = work[i, pl.ds(r, batch + 8), lanes]
                        total = x[8:, :] * taps_ref[i, pl.ds(0, 1), lanes]
                        for tap in range(1, tap_count):
                            shifted = pltpu.roll(x, tap, 0)[8:, :]
                            total = total + shifted * taps_ref[i, pl.ds(tap, 1), lanes]
                        conv.append(total)
                    work[3, pl.ds(r, batch), lanes] = conv[0]
                    signal_rows[strided(r * groups + j, batch, groups), :] = conv[1] * conv[2]

            for i in range(3):
                work[i, pl.ds(0, 8), :] = work[i, pl.ds(chunk_rows, 8), :]

            @pl.loop(0, chunk_rows // batch)
            def _(b):
                r = pl.multiple_of(b * batch, batch)
                for i in range(3):
                    work[i, pl.ds(r + 8, batch), :] = jnp.zeros((batch, width), f32)

            poles_held = [pole[pl.ds(q * groups, groups), :] for q in range(poles)]
            res_held = [residue[pl.ds(q * groups, groups), :] for q in range(poles)]
            skip_held = skip_rows[...]

            def advance(t, state):
                row = signal_rows[row_at(t), :]
                state = tuple(poles_held[q] * state[q] + row for q in range(poles))
                terms = [res_held[q] * state[q] for q in range(poles)]
                while len(terms) > 1:
                    terms = [a + b for a, b in zip(terms[::2], terms[1::2])] + terms[len(terms) // 2 * 2 :]
                signal_rows[row_at(t), :] = terms[0] + skip_held * row
                return state

            entry = tuple(state_rows[pl.ds(q * groups, groups), :] for q in range(poles))
            last = lax.fori_loop(0, chunk_rows, advance, entry, unroll=8)
            for q in range(poles):
                state_rows[pl.ds(q * groups, groups), :] = last[q]

            @pl.loop(0, groups)
            def _(j):
                lanes = pl.ds(pl.multiple_of(j * 128, 128), 128)

                @pl.loop(0, chunk_rows // batch)
                def _(b):
                    r = pl.multiple_of(b * batch, batch)
                    mixed = signal_rows[strided(r * groups + j, batch, groups), :]
                    gated[k, pl.ds(r, batch), lanes] = (work[3, pl.ds(r, batch), lanes] * mixed).astype(bf16)

            gate_copy(k).start()

        for half in range(2):
            residual_copy(half).wait_send()

        @pl.loop(0, chunks)
        def _(k):
            gate_copy(k).wait_send()
            own_part(k, finish)
            cross_start(k, finish, False)

            @pl.loop(1, line)
            def _(j):
                line_part(k, j, finish, False)
                cross_part(k, j, finish, False)

        for half in range(2):
            result_copy(half).wait_recv()
            for b in range(chunk_rows // small):
                out_ref[pl.ds(half * chunk_rows + b * small, small), :] = rows_here[half, pl.ds(b * small, small), :]

    def back():
        def flexible(k):
            return k >= chunks - 1

        def target_at(q):
            first = 1 - lax.div(q, line)
            return place(line - 1 - lax.rem(q, line)) * 2 + first * across + (1 - first) * y

        def w_copy(g):
            target = target_at(lax.rem(g, n))
            slot = lax.rem(g, W_SLOTS)
            return pltpu.make_async_copy(
                out_w_hbm.at[:, pl.ds(pl.multiple_of(target * width, 128), width)],
                w_buf.at[slot],
                w_sem.at[slot],
            )

        def multiply(k, q):
            g = k * n + q
            slot = lax.rem(g, W_SLOTS)
            w_copy(g).wait()
            work[target_at(q), pl.ds(0, chunk_rows), :] = jnp.dot(
                gated[k], w_buf[slot], preferred_element_type=f32
            )

            @pl.when(g + W_SLOTS < chunks * n)
            def _():
                w_copy(g + W_SLOTS).start()

        def send(k, block, p, dst_slot, way, device):
            return remote(
                outgoing.at[lax.rem(k, 2), block, span_of(p), :], held.at[k, dst_slot, span_of(p), :],
                way, k, block, p, device,
            )

        def sent(k, block, p):
            pltpu.make_async_remote_copy(
                src_ref=outgoing.at[lax.rem(k, 2), block, span_of(p), :], dst_ref=held.at[k, block, span_of(p), :],
                send_sem=send_sem.at[0, k, block, p], recv_sem=recv_sem.at[0, k, block, p],
                device_id=chip(z, across), device_id_type=MESH,
            ).wait_send()

        def launch(k, block, p, dst_slot, way, device):
            pltpu.make_async_remote_copy(
                src_ref=outgoing.at[lax.rem(k, 2), block, span_of(p), :], dst_ref=held.at[k, dst_slot, span_of(p), :],
                send_sem=send_sem.at[0, k, block, p], recv_sem=recv_sem.at[way, k, block, p],
                device_id=device, device_id_type=MESH,
            ).start()

        def stage(k, block, p, slots):
            @pl.loop(0, pieces[p][1] // small)
            def _(b):
                span = pl.ds(pl.multiple_of(pieces[p][0] + b * small, small), small)
                total = work[block, span, :]
                for slot in slots:
                    total = total + held[k, slot, span, :].astype(f32)
                outgoing[lax.rem(k, 2), block, span, :] = total.astype(bf16)

        def free(k, block, p):
            @pl.when(k >= 2)
            def _():
                sent(k - 2, block, p)

        def launch_line(k, target, column, beside, p):
            way = 1 - above(target)
            following = z + 1 - 2 * way
            block = target * 2 + column
            distance = (target - z) * (1 - 2 * way)
            second = way * lax.div(1, distance)
            slot = (1 - second) * block + second * (n + beside)
            launch(k, block, p, slot, way, chip(following, y))

        def first_half(k):
            gate_copy(k).wait_recv()

            @pl.loop(0, line)
            def _(q):
                target = place(line - 1 - q)
                block = target * 2 + across
                multiply(k, q)

                def over(p):
                    free(k, block, p)
                    stage(k, block, p, ())
                    launch(k, block, p, target * 2 + y, 2, chip(z, across))

                def begin(p):
                    free(k, block, p)
                    stage(k, block, p, ())
                    launch_line(k, target, across, 1, p)

                each("line", flexible(k), over)

                @pl.when(jnp.logical_and(edge, q < line - 1))
                def _():
                    each("cross", flexible(k), begin)

        def second_half(k):
            @pl.loop(0, line - 1)
            def _(q):
                target = place(line - 1 - q)
                way = 1 - above(target)
                block = target * 2 + y
                other = target * 2 + across
                multiply(k, line + q)

                def other_line(p):
                    free(k, other, p)
                    arrived(way, k, other, p)
                    stage(k, other, p, (other,))
                    launch_line(k, target, across, 1, p)

                def own_line(p):
                    free(k, block, p)

                    @pl.when(edge)
                    def _():
                        stage(k, block, p, ())

                    @pl.when(middle)
                    def _():
                        arrived(way, k, block, p)
                        stage(k, block, p, (block,))

                    launch_line(k, target, y, 0, p)

                def summed(p):
                    free(k, block, p)
                    arrived(2, k, block, p)

                    @pl.when(edge)
                    def _():
                        stage(k, block, p, (other,))

                    @pl.when(middle)
                    def _():
                        arrived(way, k, block, p)
                        stage(k, block, p, (other, block))

                    launch_line(k, target, y, 0, p)

                @pl.when(middle)
                def _():
                    each("cross", flexible(k), other_line)

                each("cross", flexible(k), own_line)
                each("line", flexible(k), summed)

            multiply(k, n - 1)
            beside = z * 2 + across

            def turn(p):
                free(k, beside, p)
                incoming(k, beside, p)
                by_ends(lambda slots: stage(k, beside, p, slots), beside, n + 1)
                launch(k, beside, p, n + 2, 2, chip(z, across))

            each("cross", flexible(k), turn)

        def incoming(k, block, p):
            @pl.when(has_low)
            def _():
                arrived(0, k, block, p)

            @pl.when(has_high)
            def _():
                arrived(1, k, block, p)

        def by_ends(act, low_slot, high_slot):
            @pl.when(middle)
            def _():
                act((low_slot, high_slot))

            @pl.when(z == 0)
            def _():
                act((high_slot,))

            @pl.when(z == line - 1)
            def _():
                act((low_slot,))

        def result(k, p, slots):
            @pl.loop(0, pieces[p][1] // small)
            def _(b):
                r = pl.multiple_of(pieces[p][0] + b * small, small)
                span = pl.ds(r, small)
                total = work[me, span, :]
                for slot in slots:
                    total = total + held[k, slot, span, :].astype(f32)
                total = (rows_here[k, span, :].astype(f32) + total).astype(bf16)

                @pl.when(k < 2)
                def _():
                    rows_here[k, span, :] = total

                @pl.when(k >= 2)
                def _():
                    out_ref[pl.ds(pl.multiple_of((k - 2) * chunk_rows + r, small), small), :] = total

        def conclude(k):
            beside = z * 2 + across

            def after_line(p):
                arrived(2, k, me, p)
                incoming(k, me, p)
                by_ends(lambda slots: result(k, p, slots + (beside,)), me, n)

            def after_cross(p):
                incoming(k, me, p)
                arrived(2, k, me, p)
                by_ends(lambda slots: result(k, p, slots + (n + 2,)), me, n)

            each("line", flexible(k), after_line)
            each("cross", flexible(k), after_cross)

            @pl.when(k < 2)
            def _():
                result_copy(k).start()

        for g in range(W_SLOTS):
            w_copy(jnp.int32(g)).start()
        own_copies = [
            pltpu.make_async_copy(tok_hbm.at[pl.ds(h * chunk_rows, chunk_rows), :], rows_here.at[2 + h], local_sem.at[h])
            for h in range(2)
        ]
        for copy in own_copies:
            copy.start()
        greet_all()
        for half in range(2):
            token_copy(half).start()
        for copy in own_copies:
            copy.wait()
        for half in range(2):
            residual_copy(half).wait_recv()

        @pl.loop(0, chunks + 1)
        def _(k):
            @pl.when(k > 0)
            def _():
                second_half(k - 1)

            @pl.when(k < chunks)
            def _():
                first_half(k)

            @pl.when(k > 0)
            def _():
                conclude(k - 1)

        for half in range(2):
            token_copy(half).wait_send()
            result_copy(half).wait_send()

        @pl.loop(chunks - 2, chunks)
        def _(k):
            @pl.loop(0, n)
            def _(block):
                @pl.when(block != me)
                def _():
                    for p in range(len(pieces)):
                        sent(k, block, p)

    @pl.when(seq == 0)
    def _():
        front()

    @pl.when(seq > 0)
    def _():
        back()


def route_pieces(chunk_rows):
    unit = 16
    total = chunk_rows // unit
    cross = max(1, total * 3 // 16)
    straight = total - 2 * cross
    counts = [(straight + 1) // 2, straight // 2, cross, cross]
    routes = ["line", "line", "either", "cross"]
    spans, at = [], 0
    for count, route in zip(counts, routes):
        if count:
            spans.append((at * unit, count * unit, route))
            at += count
    return spans


def on_grid(n, tokens, norm_gain, in_weight, short_weight, log_decay, residue, skip, out_weight):
    rows, width = tokens.shape
    groups = width // 128
    poles = log_decay.shape[0]
    chunk_rows = rows // 2
    count = len(route_pieces(chunk_rows))
    vmem = pl.BlockSpec(memory_space=pltpu.VMEM)
    anywhere = pl.BlockSpec(memory_space=pl.ANY)
    f32, bf16 = jnp.float32, jnp.bfloat16
    dma = pltpu.SemaphoreType.DMA
    return pl.pallas_call(
        functools.partial(grid_kernel, n, EPSILON),
        out_shape=jax.ShapeDtypeStruct((rows, width), bf16),
        in_specs=[anywhere, vmem, anywhere, vmem, vmem, vmem, vmem, anywhere],
        out_specs=vmem,
        scratch_shapes=[
            pltpu.VMEM((4, n + 3, chunk_rows, width), bf16),
            pltpu.VMEM((n, chunk_rows + 8, width), f32),
            pltpu.VMEM((W_SLOTS, width, width), bf16),
            pltpu.VMEM((2, n, chunk_rows, width), bf16),
            pltpu.VMEM((4, chunk_rows, width), bf16),
            pltpu.VMEM((4, chunk_rows, width), bf16),
            pltpu.VMEM((chunk_rows, width), bf16),
            pltpu.VMEM((chunk_rows, 128), f32),
            pltpu.VMEM((chunk_rows * groups, 128), f32),
            pltpu.VMEM((poles * groups, 128), f32),
            pltpu.VMEM((poles * groups, 128), f32),
            pltpu.VMEM((groups, 128), f32),
            pltpu.VMEM((poles * groups, 128), f32),
            dma((3, 4, n, count)),
            dma((3, 4, n, count)),
            dma((W_SLOTS,)),
            dma((2,)),
            dma((2,)),
            dma((2,)),
            dma((4,)),
            dma((4,)),
            dma((2,)),
            dma((2,)),
        ],
        compiler_params=pltpu.CompilerParams(
            collective_id=2, has_side_effects=True, vmem_limit_bytes=60 << 20
        ),
    )(tokens, norm_gain[None, :], in_weight, short_weight, log_decay, residue, skip[None, :], out_weight)


def per_device(n, tokens, norm_gain, in_weight, short_weight, log_decay, residue, skip, out_weight):
    rows, width = tokens.shape
    if n == 8 and rows % 64 == 0:
        return on_grid(n, tokens, norm_gain, in_weight, short_weight, log_decay, residue, skip, out_weight)
    groups = width // 128
    poles = log_decay.shape[0]
    middle = n // 2
    vmem = pl.BlockSpec(memory_space=pltpu.VMEM)
    anywhere = pl.BlockSpec(memory_space=pl.ANY)
    f32, bf16 = jnp.float32, jnp.bfloat16
    dma = pltpu.SemaphoreType.DMA
    gated = pl.pallas_call(
        functools.partial(front_kernel, n, EPSILON),
        out_shape=jax.ShapeDtypeStruct((rows, width), bf16),
        in_specs=[anywhere, vmem, anywhere, vmem, vmem, vmem, vmem],
        out_specs=vmem,
        scratch_shapes=[
            pltpu.VMEM((n, rows, width), bf16),
            pltpu.VMEM((3, rows + 8, width), f32),
            pltpu.VMEM((W_SLOTS, width, width), bf16),
            pltpu.VMEM((rows, width), bf16),
            pltpu.VMEM((rows, 128), f32),
            pltpu.VMEM((rows, width), f32),
            pltpu.VMEM((rows * groups, 128), f32),
            pltpu.VMEM((poles * groups, 128), f32),
            pltpu.VMEM((poles * groups, 128), f32),
            pltpu.VMEM((groups, 128), f32),
            pltpu.VMEM((3, 8, width), f32),
            pltpu.VMEM((3, 8, width), f32),
            pltpu.VMEM((poles * groups, 128), f32),
            pltpu.VMEM((poles * groups, 128), f32),
            pltpu.VMEM((poles * groups, 128), f32),
            dma((2, middle, PIECES)),
            dma((2, middle, PIECES)),
            dma((W_SLOTS,)),
            dma,
            dma((2,)),
            dma((2,)),
            pltpu.SemaphoreType.REGULAR,
        ],
        compiler_params=pltpu.CompilerParams(
            collective_id=0, has_side_effects=True, vmem_limit_bytes=56 << 20
        ),
    )(tokens, norm_gain[None, :], in_weight, short_weight, log_decay, residue, skip[None, :])
    return pl.pallas_call(
        functools.partial(back_kernel, n),
        out_shape=jax.ShapeDtypeStruct((rows, width), bf16),
        in_specs=[vmem, vmem, anywhere],
        out_specs=vmem,
        scratch_shapes=[
            pltpu.VMEM((W_SLOTS, width, width), bf16),
            pltpu.VMEM((2, rows, width), f32),
            pltpu.VMEM((2, middle, rows, width), bf16),
            pltpu.VMEM((2, middle, rows, width), bf16),
            dma((2, middle, PIECES)),
            dma((2, middle, PIECES)),
            dma((W_SLOTS,)),
        ],
        compiler_params=pltpu.CompilerParams(
            collective_id=1, has_side_effects=True, vmem_limit_bytes=56 << 20
        ),
    )(gated, tokens, out_weight)


def solution(mesh):
    return jax.shard_map(
        functools.partial(per_device, mesh.shape["chan"]),
        mesh=mesh,
        in_specs=(
            P(("groups", "seq"), "chan"),
            P(),
            P(None, None, "chan"),
            P(None, None, "chan"),
            P(None, "chan"),
            P(None, "chan"),
            P("chan"),
            P("chan", None),
        ),
        out_specs=P(("groups", "seq"), "chan"),
        check_vma=False,
    )
```

```python
import functools

import jax
import jax.numpy as jnp
from jax import lax
from jax.experimental import pallas as pl
from jax.experimental.pallas import tpu as pltpu
from jax.sharding import PartitionSpec as P

EPSILON = 1e-06
MESH = pl.DeviceIdType.MESH
PIECES = 4
W_SLOTS = 4
W_DEEP = 3
HALVES = (5, 6)
SIGNAL = (0, 1, 1, 2, 2, 0, 1)
STEPS = 11
TIMES = {
    "far": ((5, 3), (14, 14), (24, 19), (36, 31)),
    "own": (None, (1, 5), (9, 11), (15, 20)),
    "near": ((0, 1), (7, 8), (14, 14), (30, 27)),
    "next": ((3, 1), (10, 9), (18, 17), (30, 28)),
    "last": ((7, 6), (18, 17), (29, 25), (40, 39)),}


def ring_position(index, n):
    odd = lax.rem(index, 2)
    return (1 - odd) * lax.div(index, 2) + odd * (n - 1 - lax.div(index, 2))


def ring_index(position, n):
    back = lax.div(position, n // 2)
    return (1 - back) * (2 * position) + back * (2 * (n - 1 - position) + 1)


def greet(peers):
    barrier = pltpu.get_barrier_semaphore()
    for peer in peers:
        pl.semaphore_signal(barrier, inc=1, device_id=peer, device_id_type=MESH)
    pl.semaphore_wait(barrier, len(peers))


def strided(start, size, stride):
    return pl.ds(start, size) if stride == 1 else pl.ds(start, size, stride=stride)


def front_kernel(
    n, eps, tok_hbm, gain_ref, w_hbm, taps_ref, decay_ref, res_ref, skip_ref, gated_ref,
    held, acc, w_buf, scaled, squares, query, signal_rows, pole, residue, skip_rows,
    rim_out, rim_in, state_out, state_in, first_state, send_sem, recv_sem, w_sem, own_sem, pair_send, pair_recv, turn,
):
    rows, width = tok_hbm.shape
    middle = n // 2
    piece = rows // PIECES
    groups = width // 128
    poles = decay_ref.shape[0]
    tap_count = taps_ref.shape[1]
    chunk = min(64, rows)
    tile = min(256, width)
    me = lax.axis_index("chan")
    seq = lax.axis_index("seq")
    pos = ring_position(me, n)
    right = {"chan": ring_index(lax.rem(pos + 1, n), n)}
    left = {"chan": ring_index(lax.rem(pos + n - 1, n), n)}
    partner = {"seq": 1 - seq}
    ahead = (right, left)

    def owner_of(block):
        away = lax.div(block + 1, 2)
        odd = lax.rem(block, 2)
        return ring_index(lax.rem(pos + odd * (n - away) + (1 - odd) * away, n), n)

    def w_copy(g):
        owner = owner_of(lax.div(g, 3))
        slot = lax.rem(g, W_SLOTS)
        return pltpu.make_async_copy(
            w_hbm.at[lax.rem(g, 3), pl.ds(pl.multiple_of(owner * width, 128), width), :],
            w_buf.at[slot],
            w_sem.at[slot],
        )

    def hop(direction, step, part, away):
        shift = pos + n - away if direction == 0 else pos + away
        owner = ring_index(lax.rem(shift, n), n)
        span = pl.ds(part * piece, piece)
        return pltpu.make_async_remote_copy(
            src_ref=held.at[owner, span, :],
            dst_ref=held.at[owner, span, :],
            send_sem=send_sem.at[direction, step, part],
            recv_sem=recv_sem.at[direction, step, part],
            device_id=ahead[direction],
            device_id_type=MESH,
        )

    own = pltpu.make_async_copy(tok_hbm, held.at[me], own_sem)
    own.start()
    for g in range(W_SLOTS):
        w_copy(jnp.int32(g)).start()
    greet((right, left, partner))
    own.wait()

    @pl.when(seq > 0)
    def _():
        pl.semaphore_wait(turn, 1)

    for part in range(PIECES):
        for direction in range(2):
            hop(direction, 0, part, 0).start()

    @pl.loop(0, rows // chunk)
    def _(b):
        r = pl.multiple_of(b * chunk, chunk)
        squares[pl.ds(r, chunk), :] = jnp.zeros((chunk, 128), jnp.float32)
        for i in range(3):
            acc[i, pl.ds(r + 8, chunk), :] = jnp.zeros((chunk, width), jnp.float32)

    for j in range(groups):
        lanes = pl.ds(j * 128, 128)
        pole[strided(j, poles, groups), :] = jnp.exp(decay_ref[:, lanes])
        residue[strided(j, poles, groups), :] = res_ref[:, lanes]
        skip_rows[pl.ds(j, 1), :] = skip_ref[:, lanes]

    def prepare(block):
        owner = owner_of(block)
        gain = gain_ref[:, pl.ds(pl.multiple_of(owner * width, 128), width)]
        small = min(32, rows)

        @pl.loop(0, rows // small)
        def _(b):
            r = pl.multiple_of(b * small, small)
            x = held[owner, pl.ds(r, small), :].astype(jnp.float32)
            scaled[pl.ds(r, small), :] = (x * gain).astype(jnp.bfloat16)
            total = squares[pl.ds(r, small), :]
            for j in range(groups):
                xj = x[:, j * 128 : (j + 1) * 128]
                total = total + xj * xj
            squares[pl.ds(r, small), :] = total

    def multiply(block, i):
        g = block * 3 + i
        slot = lax.rem(g, W_SLOTS)
        w_copy(g).wait()

        @pl.loop(0, width // tile)
        def _(c):
            cols = pl.ds(pl.multiple_of(c * tile, 128), tile)
            acc[i, pl.ds(8, rows), cols] += jnp.dot(
                scaled[...], w_buf[slot, :, cols], preferred_element_type=jnp.float32
            )

        @pl.when(g + W_SLOTS < n * 3)
        def _():
            w_copy(g + W_SLOTS).start()

    def arrive(step, part):
        for direction in range(2):
            hop(direction, step - 1, part, step).wait_recv()
            if part // (PIECES // 2) == direction:
                hop(direction, step, part, step).start()
            else:

                @pl.when(step < middle - 1)
                def _():
                    hop(direction, step, part, step).start()

    def pair_part(step, quarter):
        near = 2 * step - 1
        if quarter == 0:
            prepare(near)
            multiply(near, 0)
            multiply(near, 1)
        elif quarter == 1:
            multiply(near, 2)
        elif quarter == 2:
            prepare(near + 1)
            multiply(near + 1, 0)
            multiply(near + 1, 1)
        else:
            multiply(near + 1, 2)

    for part in range(PIECES):
        arrive(jnp.int32(1), part)
        if part == 0:
            prepare(jnp.int32(0))
        if part < 3:
            multiply(jnp.int32(0), part)

    @pl.loop(2, middle)
    def _(step):
        for part in range(PIECES):
            arrive(step, part)
            pair_part(step - 1, part)

    @pl.when(seq == 0)
    def _():
        pl.semaphore_signal(turn, inc=1, device_id=partner, device_id_type=MESH)

    for part in range(PIECES):
        pair_part(jnp.int32(middle - 1), part)
    for part in range(PIECES):
        hop(part // (PIECES // 2), middle - 1, part, middle).wait_recv()
    prepare(jnp.int32(n - 1))
    for i in range(3):
        multiply(jnp.int32(n - 1), i)

    @pl.loop(0, rows // chunk)
    def _(b):
        r = pl.multiple_of(b * chunk, chunk)
        mean = jnp.sum(squares[pl.ds(r, chunk), :], axis=1, keepdims=True) / (n * width)
        inv = lax.rsqrt(mean + eps)
        for i in range(3):
            span = pl.ds(r + 8, chunk)
            acc[i, span, :] = (acc[i, span, :] * inv).astype(jnp.bfloat16).astype(jnp.float32)

    rim_out[...] = acc[:, pl.ds(rows, 8), :]
    rim = pltpu.make_async_remote_copy(
        src_ref=rim_out, dst_ref=rim_in, send_sem=pair_send.at[0], recv_sem=pair_recv.at[0],
        device_id=partner, device_id_type=MESH,
    )

    @pl.when(seq == 0)
    def _():
        rim.start()

    @pl.when(seq > 0)
    def _():
        rim.wait_recv()

    acc[:, pl.ds(0, 8), :] = jnp.zeros((3, 8, width), jnp.float32)

    @pl.when(seq > 0)
    def _():
        acc[:, pl.ds(0, 8), :] = rim_in[...]


    @pl.loop(0, groups)
    def _(j):
        lanes = pl.ds(pl.multiple_of(j * 128, 128), 128)

        @pl.loop(0, rows // chunk)
        def _(b):
            r = pl.multiple_of(b * chunk, chunk)
            conv = []
            for i in range(3):
                x = acc[i, pl.ds(r, chunk + 8), lanes]
                total = x[8:, :] * taps_ref[i, pl.ds(0, 1), lanes]
                for tap in range(1, tap_count):
                    shifted = pltpu.roll(x, tap, 0)[8:, :]
                    total = total + shifted * taps_ref[i, pl.ds(tap, 1), lanes]
                conv.append(total)
            query[pl.ds(r, chunk), lanes] = conv[0]
            signal_rows[strided(r * groups + j, chunk, groups), :] = conv[1] * conv[2]

    def row_at(t):
        return pl.ds(pl.multiple_of(t * groups, groups), groups)

    poles_held = [pole[pl.ds(k * groups, groups), :] for k in range(poles)]

    carry = pltpu.make_async_remote_copy(
        src_ref=state_out, dst_ref=state_in, send_sem=pair_send.at[1], recv_sem=pair_recv.at[1],
        device_id=partner, device_id_type=MESH,
    )
    entry_rows = poles * groups

    @pl.when(seq == 0)
    def _():
        first_state[...] = jnp.zeros((entry_rows, 128), jnp.float32)

    @pl.when(seq > 0)
    def _():
        carry.wait_recv()
        first_state[...] = state_in[...]

    res_held = [residue[pl.ds(k * groups, groups), :] for k in range(poles)]
    skip_held = skip_rows[...]

    def with_output(t, state):
        row = signal_rows[row_at(t), :]
        state = tuple(poles_held[k] * state[k] + row for k in range(poles))
        terms = [res_held[k] * state[k] for k in range(poles)]
        while len(terms) > 1:
            terms = [a + b for a, b in zip(terms[::2], terms[1::2])] + terms[len(terms) // 2 * 2 :]
        signal_rows[row_at(t), :] = terms[0] + skip_held * row
        return state

    entry = tuple(first_state[pl.ds(k * groups, groups), :] for k in range(poles))
    last = lax.fori_loop(0, rows, with_output, entry, unroll=4)
    for k in range(poles):
        state_out[pl.ds(k * groups, groups), :] = last[k]

    @pl.when(seq == 0)
    def _():
        carry.start()

    @pl.loop(0, groups)
    def _(j):
        lanes = pl.ds(pl.multiple_of(j * 128, 128), 128)

        @pl.loop(0, rows // chunk)
        def _(b):
            r = pl.multiple_of(b * chunk, chunk)
            long = signal_rows[strided(r * groups + j, chunk, groups), :]
            gated_ref[pl.ds(r, chunk), lanes] = (query[pl.ds(r, chunk), lanes] * long).astype(jnp.bfloat16)

    @pl.when(seq == 0)
    def _():
        rim.wait_send()
        carry.wait_send()

    for part in range(PIECES):
        for direction in range(2):

            @pl.loop(0, middle - 1)
            def _(step):
                hop(direction, step, part, step).wait_send()

        hop(part // (PIECES // 2), middle - 1, part, middle - 1).wait_send()


def back_kernel(
    n, gated_ref, tok_ref, w_hbm, out_ref, w_buf, partial, outgoing, incoming, send_sem, recv_sem, w_sem
):
    rows, width = tok_ref.shape
    middle = n // 2
    piece = rows // PIECES
    small = min(32, piece)
    tile = min(256, width)
    me = lax.axis_index("chan")
    pos = ring_position(me, n)
    right = {"chan": ring_index(lax.rem(pos + 1, n), n)}
    left = {"chan": ring_index(lax.rem(pos + n - 1, n), n)}
    ahead = (right, left)

    def w_copy(block):
        away = middle - lax.div(block + 1, 2)
        odd = lax.rem(block, 2)
        target = ring_index(lax.rem(pos + odd * away + (1 - odd) * (n - away), n), n)
        slot = lax.rem(block, W_SLOTS)
        return pltpu.make_async_copy(
            w_hbm.at[:, pl.ds(pl.multiple_of(target * width, 128), width)],
            w_buf.at[slot],
            w_sem.at[slot],
        )

    def hop(direction, step, part):
        span = pl.ds(part * piece, piece)
        return pltpu.make_async_remote_copy(
            src_ref=outgoing.at[direction, step, span, :],
            dst_ref=incoming.at[direction, step, span, :],
            send_sem=send_sem.at[direction, step, part],
            recv_sem=recv_sem.at[direction, step, part],
            device_id=ahead[direction],
            device_id_type=MESH,
        )

    def multiply(block, place):
        slot = lax.rem(block, W_SLOTS)
        w_copy(block).wait()

        @pl.loop(0, width // tile)
        def _(c):
            cols = pl.ds(pl.multiple_of(c * tile, 128), tile)
            partial[place, :, cols] = jnp.dot(
                gated_ref[...], w_buf[slot, :, cols], preferred_element_type=jnp.float32
            )

        @pl.when(block + W_SLOTS < n)
        def _():
            w_copy(block + W_SLOTS).start()

    def send(direction, step, part, place, add):
        @pl.loop(0, piece // small)
        def _(b):
            span = pl.ds(pl.multiple_of(part * piece + b * small, small), small)
            total = partial[place, span, :]
            if add:
                total = total + incoming[direction, step - 1, span, :].astype(jnp.float32)
            outgoing[direction, step, span, :] = total.astype(jnp.bfloat16)

        hop(direction, step, part).start()

    def side(part):
        return part // (PIECES // 2)

    order = [k // 2 + (k % 2) * (PIECES // 2) for k in range(PIECES)]
    for block in range(W_SLOTS):
        w_copy(jnp.int32(block)).start()
    greet((right, left))
    multiply(jnp.int32(0), 0)
    for part in order:
        send(side(part), 0, part, 0, False)
    for direction in range(2):
        multiply(jnp.int32(1 + direction), direction)
    for direction in range(2):
        for part in range(PIECES):
            if side(part) != direction:
                send(direction, 1, part, direction, False)
    for part in order:
        hop(side(part), 0, part).wait_recv()
        send(side(part), 1, part, side(part), True)

    @pl.loop(2, middle)
    def _(step):
        for direction in range(2):
            multiply(2 * step - 1 + direction, direction)
        for k in range(PIECES):
            for direction in range(2):
                part = (k + (1 - direction) * (PIECES // 2)) % PIECES
                hop(direction, step - 1, part).wait_recv()
                send(direction, step, part, direction, True)

    multiply(jnp.int32(n - 1), 0)
    for part in range(PIECES):
        for direction in range(2):
            hop(direction, middle - 1, part).wait_recv()

        @pl.loop(0, piece // small)
        def _(b):
            span = pl.ds(pl.multiple_of(part * piece + b * small, small), small)
            total = partial[0, span, :]
            for direction in range(2):
                total = total + incoming[direction, middle - 1, span, :].astype(jnp.float32)
            out_ref[span, :] = (tok_ref[span, :].astype(jnp.float32) + total).astype(jnp.bfloat16)

    for part in range(PIECES):
        hop(side(part), 0, part).wait_send()
        for direction in range(2):

            @pl.loop(1, middle)
            def _(step):
                hop(direction, step, part).wait_send()


def grid_kernel(
    n, eps, tok_hbm, gain_ref, in_hbm, taps_ref, decay_ref, res_ref, skip_ref, out_w_hbm, out_ref,
    held, work, pool, rows_here, proj, rim, gated, scaled, squares, signal_rows, pole, residue, skip_rows, state_rows,
    send_sem, recv_sem, w_sem, local_sem, tok_send, tok_recv, gate_send, gate_recv, back_send, back_recv, credit,
):
    rows, width = tok_hbm.shape
    chunk_rows = rows // 2
    chunks = 4
    line = n // 2
    groups = width // 128
    poles = decay_ref.shape[0]
    tap_count = taps_ref.shape[1]
    small = 16
    batch = min(64, chunk_rows)
    f32, bf16 = jnp.float32, jnp.bfloat16
    pieces = route_pieces(chunk_rows)
    me = lax.axis_index("chan")
    seq = lax.axis_index("seq")
    z = lax.div(me, 2)
    y = lax.rem(me, 2)
    across = 1 - y
    partner = {"seq": 1 - seq}
    has_low = z > 0
    has_high = z < line - 1
    edge = jnp.logical_or(z == 0, z == line - 1)
    middle = jnp.logical_and(has_low, has_high)
    mid = lax.div(z * (3 - z), 2)
    high = lax.div(z, 2)

    def place(j):
        wrap = lax.div(j, 3)
        near = (1 - mid) * j + mid * ((1 - wrap) * lax.rem(j + 1, 3) + 3 * wrap)
        return (1 - high) * near + high * (3 - near)

    def above(target):
        return lax.div(target - z + 3, 4)

    def chip(row, column):
        return {"chan": row * 2 + column}

    def span_of(p):
        return pl.ds(pieces[p][0], pieces[p][1])

    def w_rows(slot):
        return pool.at[pl.ds(pl.multiple_of(slot * width, small), width), :]

    def out_rows(k, block, start, size):
        at = W_SLOTS * width + (lax.rem(k, 2) * n + block) * chunk_rows + start
        return pl.ds(pl.multiple_of(at, small), size)

    def each(kind, flexible, act):
        longer, shorter = (2, 1) if kind == "line" else (4, 3)
        if kind == "line":
            act(0)

        @pl.when(flexible)
        def _():
            act(longer)

        @pl.when(jnp.logical_not(flexible))
        def _():
            act(shorter)

    def remote(src, dst, way, k, block, p, device):
        return pltpu.make_async_remote_copy(
            src_ref=src, dst_ref=dst, send_sem=send_sem.at[way, k, block, SIGNAL[p]],
            recv_sem=recv_sem.at[way, k, block, SIGNAL[p]], device_id=device, device_id_type=MESH,
        )

    def arrived(way, k, block, p):
        here = held.at[k, block, span_of(p), :]
        remote(here, here, way, k, block, p, chip(z, across)).wait_recv()

    def token_copy(half):
        return pltpu.make_async_remote_copy(
            src_ref=tok_hbm.at[pl.ds(half * chunk_rows, chunk_rows), :],
            dst_ref=held.at[2 + half, me],
            send_sem=tok_send.at[half], recv_sem=tok_recv.at[half], device_id=partner, device_id_type=MESH,
        )

    def residual_copy(half):
        return pltpu.make_async_remote_copy(
            src_ref=tok_hbm.at[pl.ds(half * chunk_rows, chunk_rows), :],
            dst_ref=rows_here.at[half],
            send_sem=tok_send.at[half], recv_sem=tok_recv.at[half], device_id=partner, device_id_type=MESH,
        )

    def gate_copy(k):
        here = proj.at[lax.rem(k, 2), :, pl.ds(16, chunk_rows), :]
        return pltpu.make_async_remote_copy(
            src_ref=here, dst_ref=here, send_sem=gate_send.at[k], recv_sem=gate_recv.at[k],
            device_id=partner, device_id_type=MESH,
        )

    def result_copy(k):
        return pltpu.make_async_remote_copy(
            src_ref=rows_here.at[k], dst_ref=rows_here.at[k], send_sem=back_send.at[k], recv_sem=back_recv.at[k],
            device_id=partner, device_id_type=MESH,
        )

    def greet_all():
        barrier = pltpu.get_barrier_semaphore()

        def hello(device):
            pl.semaphore_signal(barrier, inc=1, device_id=device, device_id_type=MESH)

        hello(partner)
        hello(chip(z, across))

        @pl.when(has_low)
        def _():
            hello(chip(z - 1, y))

        @pl.when(has_high)
        def _():
            hello(chip(z + 1, y))

        pl.semaphore_wait(barrier, 3 + mid)

    def front():
        def flexible(k):
            return k < 2

        def block_at(s):
            even = 1 - lax.rem(s, 2)
            last = lax.div(s, n - 1)
            other = even * lax.div(s + n - 1, n) + last
            own = lax.div(s + 1, 2)
            beside = even * (lax.div(s, 2) - 1) + 3 * last
            j = (1 - other) * own + other * beside
            return place(j) * 2 + (1 - other) * y + other * across

        def w_copy(step, i):
            owner = block_at(lax.rem(step, n))
            slot = lax.rem(step, W_DEEP) * 3 + i
            return pltpu.make_async_copy(
                in_hbm.at[i, pl.ds(pl.multiple_of(owner * width, 128), width), :],
                w_rows(slot),
                w_sem.at[slot],
            )

        def push(way, k, block, p):
            here = held.at[k, block, span_of(p), :]
            device = (chip(z + 1, y), chip(z - 1, y), chip(z, across))[way]
            return remote(here, here, way, k, block, p, device)

        def along(way, k, block, p):
            here = held.at[k, block, span_of(p), :]
            return remote(here, here, way, k, block, p, chip(z + 1 - 2 * way, y))

        def onward(way):
            following = z + 1 - 2 * way
            return jnp.logical_and(following >= 0, following < line)

        def both_ways(k, block, p, act):
            @pl.when(has_low)
            def _():
                act(push(1, k, block, p))

            @pl.when(has_high)
            def _():
                act(push(0, k, block, p))

        def first_part():
            def leave(way, device, p):
                k = jnp.int32(0)
                remote(tok_hbm.at[span_of(p), :], held.at[k, me, span_of(p), :], way, k, me, p, device).start()

            leave(2, chip(z, across), 4)
            for p in HALVES:

                @pl.when(has_low)
                def _():
                    leave(1, chip(z - 1, y), p)

                @pl.when(has_high)
                def _():
                    leave(0, chip(z + 1, y), p)

            leave(2, chip(z, across), 0)
            leave(2, chip(z, across), 2)

        def own_part(k, act):
            each("cross", flexible(k), lambda p: act(push(2, k, me, p)))
            for p in HALVES:
                both_ways(k, me, p, act)
            each("line", flexible(k), lambda p: act(push(2, k, me, p)))

        def line_part(k, j, act, wait):
            target = place(j)
            way = above(target)
            block = target * 2 + y
            def pass_on(p):
                if wait:
                    arrived(way, k, block, p)

                @pl.when(onward(way))
                def _():
                    act(along(way, k, block, p))

            pass_on(HALVES[0])

            def after(p):
                if p > 0:
                    pass_on(HALVES[1])
                act(push(2, k, block, p))

            each("line", flexible(k), after)

        def cross_part(k, j, act, wait):
            target = place(j)
            way = above(target)
            block = target * 2 + across

            def second(p):
                if wait:
                    arrived(way, k, block, p)

                @pl.when(onward(way))
                def _():
                    act(along(way, k, block, p))

            each("cross", flexible(k), second)

        def cross_start(k, act, wait):
            block = z * 2 + across

            def second(p):
                if wait:
                    arrived(2, k, block, p)
                both_ways(k, block, p, act)

            each("cross", flexible(k), second)

        def start(copy):
            copy.start()

        def finish(copy):
            copy.wait_send()

        own_copies = [
            pltpu.make_async_copy(tok_hbm.at[pl.ds(h * chunk_rows, chunk_rows), :], held.at[h, me], local_sem.at[h])
            for h in range(2)
        ]
        for copy in own_copies:
            copy.start()
        for step in range(W_DEEP):
            for i in range(3):
                w_copy(jnp.int32(step), i).start()
        greet_all()
        first_part()
        own_copies[0].wait()
        for half in range(2):
            residual_copy(half).start()
        own_copies[1].wait()

        work[pl.ds(0, 3), :, :] = jnp.zeros((3, chunk_rows, width), f32)
        squares[...] = jnp.zeros((chunk_rows, 128), f32)
        for half in range(2):
            token_copy(half).wait_recv()

        def near_part(k):
            line_part(k, jnp.int32(1), start, True)
            cross_start(k, start, True)

        def next_part(k):
            line_part(k, jnp.int32(2), start, True)
            cross_part(k, jnp.int32(1), start, True)

        def far_part(k):
            line_part(k, jnp.int32(3), start, True)
            cross_part(k, jnp.int32(2), start, True)

        def last_part(k):
            cross_part(k, jnp.int32(3), start, True)

        def ahead_part(k):
            own_part(k, start)

        acts = {"far": far_part, "own": ahead_part, "near": near_part, "next": next_part, "last": last_part}

        def relay(k, at, spots):
            step = k * STEPS + at
            for name, act in acts.items():
                chosen = jnp.int32(0)
                used = False
                for chunk, when in enumerate(TIMES[name]):
                    if when is None or not any(t % STEPS in spots for t in when):
                        continue
                    used = True
                    chosen = chosen + jnp.where(step == when[0] + mid * (when[1] - when[0]), chunk + 1, 0)
                if used:

                    @pl.when(chosen > 0)
                    def _():
                        act(chosen - 1)

        @pl.loop(0, chunks)
        def _(k):
            @pl.loop(0, n)
            def _(s):
                relay(k, s, range(n))
                odd = lax.rem(s, 2)

                @pl.when(jnp.logical_and(odd == 0, s > 0))
                def _():
                    each("line", flexible(k), lambda p: arrived(2, k, place(lax.div(s, 2) - 1) * 2 + across, p))

                @pl.when(s == n - 1)
                def _():
                    each("line", flexible(k), lambda p: arrived(2, k, place(jnp.int32(3)) * 2 + across, p))

                owner = block_at(s)
                gain = gain_ref[:, pl.ds(pl.multiple_of(owner * width, 128), width)]
                part = min(32, chunk_rows)

                @pl.loop(0, chunk_rows // part)
                def _(b):
                    r = pl.multiple_of(b * part, part)
                    x = held[k, owner, pl.ds(r, part), :].astype(f32)
                    scaled[pl.ds(r, part), :] = (x * gain).astype(bf16)
                    total = squares[pl.ds(r, part), :]
                    for j in range(groups):
                        xj = x[:, j * 128 : (j + 1) * 128]
                        total = total + xj * xj
                    squares[pl.ds(r, part), :] = total

                step = k * n + s
                for i in range(3):
                    w_copy(step, i).wait()
                for i in range(3):
                    slot = lax.rem(step, W_DEEP) * 3 + i
                    work[i] += jnp.dot(
                        scaled[...], w_rows(slot)[...], preferred_element_type=f32
                    )

                @pl.when(step + W_DEEP < chunks * n)
                def _():
                    for i in range(3):
                        w_copy(step + W_DEEP, i).start()

            relay(k, n, (n,))

            @pl.when(k >= 2)
            def _():
                gate_copy(k - 2).wait_send()

            @pl.loop(0, chunk_rows // batch)
            def _(b):
                r = pl.multiple_of(b * batch, batch)
                mean = jnp.sum(squares[pl.ds(r, batch), :], axis=1, keepdims=True) / (n * width)
                inv = lax.rsqrt(mean + eps)
                for i in range(3):
                    span = pl.ds(r, batch)
                    proj[lax.rem(k, 2), i, pl.ds(r + 16, batch), :] = (work[i, span, :] * inv).astype(bf16)
                    work[i, span, :] = jnp.zeros((batch, width), f32)
                squares[pl.ds(r, batch), :] = jnp.zeros((batch, 128), f32)

            @pl.when(k >= 2)
            def _():
                pl.semaphore_wait(credit, 1)

            gate_copy(k).start()

            relay(k, n + 1, (n + 1,))

            relay(k, n + 2, (n + 2,))

        for half in range(2):
            residual_copy(half).wait_send()

        for k in range(chunks - 2, chunks):
            gate_copy(k).wait_send()

        @pl.loop(0, chunks)
        def _(k):
            own_part(k, finish)
            cross_start(k, finish, False)

            @pl.loop(1, line)
            def _(j):
                line_part(k, j, finish, False)
                cross_part(k, j, finish, False)

        for half in range(2):
            result_copy(half).wait_recv()
            for b in range(chunk_rows // small):
                out_ref[pl.ds(half * chunk_rows + b * small, small), :] = rows_here[half, pl.ds(b * small, small), :]

    def back():
        def flexible(k):
            return k >= chunks - 1

        def target_at(q):
            last = lax.div(q, n - 1)
            over = lax.div(n - 1 - q, n - 1) + lax.rem(q, 2) * (1 - last)
            turn = over * lax.div(q + 1, 2) + (1 - over) * lax.div(q - 1, 2)
            return place(line - 1 - turn) * 2 + over * across + (1 - over) * y

        def w_copy(g):
            target = target_at(lax.rem(g, n))
            slot = lax.rem(g, W_SLOTS)
            return pltpu.make_async_copy(
                out_w_hbm.at[:, pl.ds(pl.multiple_of(target * width, 128), width)],
                w_rows(slot),
                w_sem.at[slot],
            )

        def multiply(k, q):
            g = k * n + q
            slot = lax.rem(g, W_SLOTS)
            w_copy(g).wait()
            work[target_at(q)] = jnp.dot(
                gated[...], w_rows(slot)[...], preferred_element_type=f32
            )

            @pl.when(g + W_SLOTS < chunks * n)
            def _():
                w_copy(g + W_SLOTS).start()

        def sent(k, block, p):
            pltpu.make_async_remote_copy(
                src_ref=pool.at[out_rows(k, block, *pieces[p][:2]), :], dst_ref=held.at[k, block, span_of(p), :],
                send_sem=send_sem.at[0, k, block, SIGNAL[p]], recv_sem=recv_sem.at[0, k, block, SIGNAL[p]],
                device_id=chip(z, across), device_id_type=MESH,
            ).wait_send()

        def launch(k, block, p, dst_slot, way, device):
            pltpu.make_async_remote_copy(
                src_ref=pool.at[out_rows(k, block, *pieces[p][:2]), :], dst_ref=held.at[k, dst_slot, span_of(p), :],
                send_sem=send_sem.at[0, k, block, SIGNAL[p]], recv_sem=recv_sem.at[way, k, block, SIGNAL[p]],
                device_id=device, device_id_type=MESH,
            ).start()

        def stage(k, block, p, slots):
            size = 2 * small if pieces[p][1] % (2 * small) == 0 else small

            @pl.loop(0, pieces[p][1] // size)
            def _(b):
                start = pl.multiple_of(pieces[p][0] + b * size, small)
                span = pl.ds(start, size)
                total = work[block, span, :]
                for slot in slots:
                    total = total + held[k, slot, span, :].astype(f32)
                pool[out_rows(k, block, start, size), :] = total.astype(bf16)

        def all_sent(k):
            @pl.loop(0, n)
            def _(block):
                @pl.when(block != me)
                def _():
                    each("line", flexible(k), lambda p: sent(k, block, p))
                    each("cross", flexible(k), lambda p: sent(k, block, p))

        def launch_line(k, target, column, beside, p):
            way = 1 - above(target)
            following = z + 1 - 2 * way
            block = target * 2 + column
            distance = (target - z) * (1 - 2 * way)
            second = way * lax.div(1, distance)
            slot = (1 - second) * block + second * (n + beside)
            launch(k, block, p, slot, way, chip(following, y))

        def row_at(t):
            return pl.ds(pl.multiple_of(t * groups, groups), groups)

        def mix(k):
            gate_copy(k).wait_recv()
            slot = lax.rem(k, 2)
            kept = lax.rem(z + 1, line) * 2 + y
            proj[slot, :, pl.ds(0, 16), :] = rim[...]

            @pl.loop(0, groups)
            def _(j):
                lanes = pl.ds(pl.multiple_of(j * 128, 128), 128)

                @pl.loop(0, chunk_rows // batch)
                def _(b):
                    r = pl.multiple_of(b * batch, batch)
                    conv = []
                    for i in range(3):
                        x = proj[slot, i, pl.ds(r, batch + 16), lanes].astype(f32)
                        total = x[16:, :] * taps_ref[i, pl.ds(0, 1), lanes]
                        for tap in range(1, tap_count):
                            shifted = pltpu.roll(x, tap, 0)[16:, :]
                            total = total + shifted * taps_ref[i, pl.ds(tap, 1), lanes]
                        conv.append(total)
                    work[kept, pl.ds(r, batch), lanes] = conv[0]
                    signal_rows[strided(r * groups + j, batch, groups), :] = conv[1] * conv[2]

            rim[...] = proj[slot, :, pl.ds(chunk_rows, 16), :]

            @pl.when(k < chunks - 2)
            def _():
                pl.semaphore_signal(credit, inc=1, device_id=partner, device_id_type=MESH)

            poles_held = [pole[pl.ds(q * groups, groups), :] for q in range(poles)]
            res_held = [residue[pl.ds(q * groups, groups), :] for q in range(poles)]
            skip_held = skip_rows[...]

            def advance(t, state):
                row = signal_rows[row_at(t), :]
                state = tuple(poles_held[q] * state[q] + row for q in range(poles))
                terms = [res_held[q] * state[q] for q in range(poles)]
                while len(terms) > 1:
                    terms = [a + b for a, b in zip(terms[::2], terms[1::2])] + terms[len(terms) // 2 * 2 :]
                signal_rows[row_at(t), :] = terms[0] + skip_held * row
                return state

            entry = tuple(state_rows[pl.ds(q * groups, groups), :] for q in range(poles))
            last = lax.fori_loop(0, chunk_rows, advance, entry, unroll=8)
            for q in range(poles):
                state_rows[pl.ds(q * groups, groups), :] = last[q]

            @pl.loop(0, groups)
            def _(j):
                lanes = pl.ds(pl.multiple_of(j * 128, 128), 128)

                @pl.loop(0, chunk_rows // batch)
                def _(b):
                    r = pl.multiple_of(b * batch, batch)
                    mixed = signal_rows[strided(r * groups + j, batch, groups), :]
                    gated[pl.ds(r, batch), lanes] = (work[kept, pl.ds(r, batch), lanes] * mixed).astype(bf16)

        def first_half(k):
            mix(k)

            @pl.when(k >= 2)
            def _():
                all_sent(k - 2)

            @pl.loop(0, line)
            def _(q):
                send_across(k, q)

                @pl.when(q > 0)
                def _():
                    send_line(k, q - 1)

        def send_across(k, q):
            target = place(line - 1 - q)
            block = target * 2 + across
            multiply(k, 2 * q - 1 + lax.div(line - q, line))

            def over(p):
                stage(k, block, p, ())
                launch(k, block, p, target * 2 + y, 2, chip(z, across))

            def begin(p):
                stage(k, block, p, ())
                launch_line(k, target, across, 1, p)

            each("line", flexible(k), over)

            @pl.when(jnp.logical_and(edge, q < line - 1))
            def _():
                each("cross", flexible(k), begin)

        def send_line(k, q):
            target = place(line - 1 - q)
            way = 1 - above(target)
            block = target * 2 + y
            other = target * 2 + across
            multiply(k, 2 * q + 2)

            def other_line(p):
                arrived(way, k, other, p)
                stage(k, other, p, (other,))
                launch_line(k, target, across, 1, p)

            def own_line(p):

                @pl.when(edge)
                def _():
                    stage(k, block, p, ())

                @pl.when(middle)
                def _():
                    arrived(way, k, block, p)
                    stage(k, block, p, (block,))

                launch_line(k, target, y, 0, p)

            def summed(p):
                arrived(2, k, block, p)

                @pl.when(edge)
                def _():
                    stage(k, block, p, (other,))

                @pl.when(middle)
                def _():
                    arrived(way, k, block, p)
                    stage(k, block, p, (other, block))

                launch_line(k, target, y, 0, p)

            @pl.when(middle)
            def _():
                each("cross", flexible(k), other_line)

            each("cross", flexible(k), own_line)
            each("line", flexible(k), summed)

        def last_turn(k):
            multiply(k, n - 1)
            beside = z * 2 + across

            def turn(p):
                incoming(k, beside, p)
                by_ends(lambda slots: stage(k, beside, p, slots), beside, n + 1)
                launch(k, beside, p, n + 2, 2, chip(z, across))

            each("cross", flexible(k), turn)

        def incoming(k, block, p):
            @pl.when(has_low)
            def _():
                arrived(0, k, block, p)

            @pl.when(has_high)
            def _():
                arrived(1, k, block, p)

        def by_ends(act, low_slot, high_slot):
            @pl.when(middle)
            def _():
                act((low_slot, high_slot))

            @pl.when(z == 0)
            def _():
                act((high_slot,))

            @pl.when(z == line - 1)
            def _():
                act((low_slot,))

        def result(k, p, slots):
            @pl.loop(0, pieces[p][1] // small)
            def _(b):
                r = pl.multiple_of(pieces[p][0] + b * small, small)
                span = pl.ds(r, small)
                total = work[me, span, :]
                for slot in slots:
                    total = total + held[k, slot, span, :].astype(f32)
                total = (rows_here[k, span, :].astype(f32) + total).astype(bf16)

                @pl.when(k < 2)
                def _():
                    rows_here[k, span, :] = total

                @pl.when(k >= 2)
                def _():
                    out_ref[pl.ds(pl.multiple_of((k - 2) * chunk_rows + r, small), small), :] = total

        def conclude(k):
            beside = z * 2 + across

            def after_line(p):
                arrived(2, k, me, p)
                incoming(k, me, p)
                by_ends(lambda slots: result(k, p, slots + (beside,)), me, n)

            def after_cross(p):
                incoming(k, me, p)
                arrived(2, k, me, p)
                by_ends(lambda slots: result(k, p, slots + (n + 2,)), me, n)

            each("line", flexible(k), after_line)
            each("cross", flexible(k), after_cross)

            @pl.when(k < 2)
            def _():
                result_copy(k).start()

        for g in range(W_SLOTS):
            w_copy(jnp.int32(g)).start()
        own_copies = [
            pltpu.make_async_copy(tok_hbm.at[pl.ds(h * chunk_rows, chunk_rows), :], rows_here.at[2 + h], local_sem.at[h])
            for h in range(2)
        ]
        for copy in own_copies:
            copy.start()
        greet_all()
        for half in range(2):
            token_copy(half).start()
        rim[...] = jnp.zeros((3, 16, width), bf16)
        state_rows[...] = jnp.zeros((poles * groups, 128), f32)
        for j in range(groups):
            lanes = pl.ds(j * 128, 128)
            pole[strided(j, poles, groups), :] = jnp.exp(decay_ref[:, lanes])
            residue[strided(j, poles, groups), :] = res_ref[:, lanes]
            skip_rows[pl.ds(j, 1), :] = skip_ref[:, lanes]
        for copy in own_copies:
            copy.wait()
        for half in range(2):
            residual_copy(half).wait_recv()

        @pl.loop(0, chunks + 1)
        def _(k):
            @pl.when(k < chunks)
            def _():
                first_half(k)

            @pl.when(k > 0)
            def _():
                conclude(k - 1)

            @pl.when(k < chunks)
            def _():
                last_turn(k)

        for half in range(2):
            token_copy(half).wait_send()
            result_copy(half).wait_send()

        @pl.loop(chunks - 2, chunks)
        def _(k):
            all_sent(k)

    @pl.when(seq == 0)
    def _():
        front()

    @pl.when(seq > 0)
    def _():
        back()


def route_pieces(chunk_rows):
    unit = 16
    total = chunk_rows // unit
    cross = max(1, total * 3 // 16)
    first = max(1, total * 6 // 16) * unit
    longer, shorter = (total - cross) * unit, (total - 2 * cross) * unit
    half = chunk_rows // 2
    return [
        (0, first), (first, shorter - first), (first, longer - first),
        (shorter, chunk_rows - shorter), (longer, chunk_rows - longer), (0, half), (half, half),
    ]


def on_grid(n, tokens, norm_gain, in_weight, short_weight, log_decay, residue, skip, out_weight):
    rows, width = tokens.shape
    groups = width // 128
    poles = log_decay.shape[0]
    chunk_rows = rows // 2
    vmem = pl.BlockSpec(memory_space=pltpu.VMEM)
    anywhere = pl.BlockSpec(memory_space=pl.ANY)
    f32, bf16 = jnp.float32, jnp.bfloat16
    dma = pltpu.SemaphoreType.DMA
    return pl.pallas_call(
        functools.partial(grid_kernel, n, EPSILON),
        out_shape=jax.ShapeDtypeStruct((rows, width), bf16),
        in_specs=[anywhere, vmem, anywhere, vmem, vmem, vmem, vmem, anywhere],
        out_specs=vmem,
        scratch_shapes=[
            pltpu.VMEM((4, n + 3, chunk_rows, width), bf16),
            pltpu.VMEM((n, chunk_rows, width), f32),
            pltpu.VMEM((max(3 * W_DEEP * width, W_SLOTS * width + 2 * n * chunk_rows), width), bf16),
            pltpu.VMEM((4, chunk_rows, width), bf16),
            pltpu.VMEM((2, 3, chunk_rows + 16, width), bf16),
            pltpu.VMEM((3, 16, width), bf16),
            pltpu.VMEM((chunk_rows, width), bf16),
            pltpu.VMEM((chunk_rows, width), bf16),
            pltpu.VMEM((chunk_rows, 128), f32),
            pltpu.VMEM((chunk_rows * groups, 128), f32),
            pltpu.VMEM((poles * groups, 128), f32),
            pltpu.VMEM((poles * groups, 128), f32),
            pltpu.VMEM((groups, 128), f32),
            pltpu.VMEM((poles * groups, 128), f32),
            dma((3, 4, n, 3)),
            dma((3, 4, n, 3)),
            dma((3 * W_DEEP,)),
            dma((2,)),
            dma((2,)),
            dma((2,)),
            dma((4,)),
            dma((4,)),
            dma((2,)),
            dma((2,)),
            pltpu.SemaphoreType.REGULAR,
        ],
        compiler_params=pltpu.CompilerParams(
            collective_id=2, has_side_effects=True, vmem_limit_bytes=60 << 20
        ),
    )(tokens, norm_gain[None, :], in_weight, short_weight, log_decay, residue, skip[None, :], out_weight)


def per_device(n, tokens, norm_gain, in_weight, short_weight, log_decay, residue, skip, out_weight):
    rows, width = tokens.shape
    if n == 8 and rows % 64 == 0:
        return on_grid(n, tokens, norm_gain, in_weight, short_weight, log_decay, residue, skip, out_weight)
    groups = width // 128
    poles = log_decay.shape[0]
    middle = n // 2
    vmem = pl.BlockSpec(memory_space=pltpu.VMEM)
    anywhere = pl.BlockSpec(memory_space=pl.ANY)
    f32, bf16 = jnp.float32, jnp.bfloat16
    dma = pltpu.SemaphoreType.DMA
    gated = pl.pallas_call(
        functools.partial(front_kernel, n, EPSILON),
        out_shape=jax.ShapeDtypeStruct((rows, width), bf16),
        in_specs=[anywhere, vmem, anywhere, vmem, vmem, vmem, vmem],
        out_specs=vmem,
        scratch_shapes=[
            pltpu.VMEM((n, rows, width), bf16),
            pltpu.VMEM((3, rows + 8, width), f32),
            pltpu.VMEM((W_SLOTS, width, width), bf16),
            pltpu.VMEM((rows, width), bf16),
            pltpu.VMEM((rows, 128), f32),
            pltpu.VMEM((rows, width), f32),
            pltpu.VMEM((rows * groups, 128), f32),
            pltpu.VMEM((poles * groups, 128), f32),
            pltpu.VMEM((poles * groups, 128), f32),
            pltpu.VMEM((groups, 128), f32),
            pltpu.VMEM((3, 8, width), f32),
            pltpu.VMEM((3, 8, width), f32),
            pltpu.VMEM((poles * groups, 128), f32),
            pltpu.VMEM((poles * groups, 128), f32),
            pltpu.VMEM((poles * groups, 128), f32),
            dma((2, middle, PIECES)),
            dma((2, middle, PIECES)),
            dma((W_SLOTS,)),
            dma,
            dma((2,)),
            dma((2,)),
            pltpu.SemaphoreType.REGULAR,
        ],
        compiler_params=pltpu.CompilerParams(
            collective_id=0, has_side_effects=True, vmem_limit_bytes=56 << 20
        ),
    )(tokens, norm_gain[None, :], in_weight, short_weight, log_decay, residue, skip[None, :])
    return pl.pallas_call(
        functools.partial(back_kernel, n),
        out_shape=jax.ShapeDtypeStruct((rows, width), bf16),
        in_specs=[vmem, vmem, anywhere],
        out_specs=vmem,
        scratch_shapes=[
            pltpu.VMEM((W_SLOTS, width, width), bf16),
            pltpu.VMEM((2, rows, width), f32),
            pltpu.VMEM((2, middle, rows, width), bf16),
            pltpu.VMEM((2, middle, rows, width), bf16),
            dma((2, middle, PIECES)),
            dma((2, middle, PIECES)),
            dma((W_SLOTS,)),
        ],
        compiler_params=pltpu.CompilerParams(
            collective_id=1, has_side_effects=True, vmem_limit_bytes=56 << 20
        ),
    )(gated, tokens, out_weight)


def solution(mesh):
    return jax.shard_map(
        functools.partial(per_device, mesh.shape["chan"]),
        mesh=mesh,
        in_specs=(
            P(("groups", "seq"), "chan"),
            P(),
            P(None, None, "chan"),
            P(None, None, "chan"),
            P(None, "chan"),
            P(None, "chan"),
            P("chan"),
            P("chan", None),
        ),
        out_specs=P(("groups", "seq"), "chan"),
        check_vma=False,
    )
```
